32 devices in a mesh: tm: 8 (over z, y), grp: 4 (over x, core).
Axes of the slice: x: 2, y: 2, z: 4, core: 2. Of those that a mesh axis runs over, the one named last changes fastest.
Arguments:
- features: bfloat16 [4, 8192, 512], P('grp', 'tm'), may hold values from -6 to 6
- conv5_weight: bfloat16 [1536, 512], replicated, may hold values from -0.15625 to 0.15625
- conv6_weight: bfloat16 [1024, 512], replicated, may hold values from -0.1875 to 0.1875
- conv7_weight: bfloat16 [1024, 512], replicated, may hold values from -0.1875 to 0.1875
- conv5_gain: float32 [512], replicated, may hold values from 0.25 to 1.75
- conv6_gain: float32 [512], replicated, may hold values from 0.25 to 1.75
- conv7_gain: float32 [512], replicated, may hold values from 0.25 to 1.75
- proj_gain: float32 [512], replicated, may hold values from 0.25 to 1.75
- proj_weight: bfloat16 [512, 1280], replicated, may hold values from -0.25 to 0.25
- proj_bias: float32 [1280], replicated, may hold values from -3 to 3
- pos_weight: bfloat16 [16, 128, 80, 80], P('grp'), may hold values from -0.0625 to 0.0625
- pos_bias: float32 [1280], P('grp'), may hold values from -3 to 3
- out_gain: float32 [1280], P('grp'), may hold values from 0.25 to 1.75
- out_bias: float32 [1280], P('grp'), may hold values from -3 to 3
- lengths: int32 [4], P('grp'), may hold values from 512 to 1024
- crops: int32 [4], P('grp'), may hold values from 0 to 511
Outputs:
- encoded: bfloat16 [4, 1024, 1280], P(None, 'tm', 'grp')
The draws below stay inside these ranges and needn't reach their ends.
All inputs are finite; a program needn't handle non-finite values.
Results may differ from the reference program's by a relative error of at most 0.0067.
Values may be sent and summed in bfloat16 or wider, within the bound.
No kernel may reach another device: no remote copies, remote signals or barrier semaphores. Data moves between devices by JAX's collectives and lax.ppermute only.
A program may use at most 128 MiB of HBM per device.

```python
import jax
import jax.numpy as jnp
from jax import lax

C0 = 512
D = 1280
GROUPS = 16
KPOS = 128
GW = 80
FRAMES = 1024
REC = 4


def plant(result, key, smallest, high):
    shape = result.shape
    spot = [jax.random.randint(jax.random.fold_in(key, axis), (), 0, shape[axis]) for axis in range(len(shape))]
    result = result.at[tuple(spot)].set(smallest)
    longest = shape.index(max(shape))
    spot[longest] = (spot[longest] + 1) % shape[longest]
    return result.at[tuple(spot)].set(high)


def block_scale(rng, shape, shards, least, largest):
    def one(axis_at, blocks):
        heights = jax.random.uniform(jax.random.fold_in(jax.random.fold_in(rng, 6), axis_at), (blocks,), jnp.float32, least / len(shards), largest / len(shards))
        return jnp.repeat(jnp.exp(heights), shape[axis_at] // blocks).reshape((-1,) + (1,) * (len(shape) - axis_at - 1))

    level = one(*shards[0])
    for cut in shards[1:]:
        level = level * one(*cut)
    return level


def noise(own_key, dims, deviation, reach, cuts=(), held_as=jnp.bfloat16):
    level = block_scale(own_key, dims, cuts, -0.22, 0.18) if cuts else 1.0
    result = jax.random.normal(own_key, dims, jnp.float32) * deviation * level
    return jnp.minimum(jnp.maximum(result, -reach), reach).astype(held_as)


def setup_inputs(seed: int = 0) -> dict:
    splits = jax.random.split(jax.random.key(seed), 17)
    features = noise(splits[0], (REC, 8 * FRAMES, C0), 1.0, 6.0, ((0, 4), (1, 8)))
    conv5_weight = noise(splits[1], (3 * C0, C0), (3 * C0) ** -0.5, 0.15625)
    conv6_weight = noise(splits[2], (2 * C0, C0), (2 * C0) ** -0.5, 0.1875)
    conv7_weight = noise(splits[3], (2 * C0, C0), (2 * C0) ** -0.5, 0.1875)
    conv5_gain = jnp.clip(1.0 + 0.15 * jax.random.normal(splits[4], (C0,), jnp.float32), 0.25, 1.75)
    conv6_gain = jnp.clip(1.0 + 0.15 * jax.random.normal(splits[5], (C0,), jnp.float32), 0.25, 1.75)
    conv7_gain = jnp.clip(1.0 + 0.15 * jax.random.normal(splits[6], (C0,), jnp.float32), 0.25, 1.75)
    proj_gain = jnp.clip(1.0 + 0.15 * jax.random.normal(splits[7], (C0,), jnp.float32), 0.25, 1.75)
    proj_weight = noise(splits[8], (C0, D), C0 ** -0.5, 0.25)
    proj_bias = noise(splits[9], (D,), 0.5, 3.0, (), jnp.float32)
    pos_weight = noise(splits[10], (GROUPS, KPOS, GW, GW), (KPOS * GW) ** -0.5, 0.0625, ((0, 4),))
    pos_bias = noise(splits[11], (D,), 0.5, 3.0, ((0, 4),), jnp.float32)
    out_gain = jnp.clip(1.0 + 0.15 * jax.random.normal(splits[12], (D,), jnp.float32), 0.25, 1.75)
    out_bias = noise(splits[13], (D,), 0.5, 3.0, ((0, 4),), jnp.float32)
    lengths = plant(jax.random.randint(splits[14], (REC,), FRAMES // 2, FRAMES + 1), jax.random.fold_in(splits[14], 1), FRAMES // 2, FRAMES).astype(jnp.int32)
    crops = plant(jax.random.randint(splits[15], (REC,), 0, FRAMES // 2), jax.random.fold_in(splits[15], 1), 0, (FRAMES // 2) - 1).astype(jnp.int32)
    return dict(features=features, conv5_weight=conv5_weight, conv6_weight=conv6_weight, conv7_weight=conv7_weight, conv5_gain=conv5_gain, conv6_gain=conv6_gain, conv7_gain=conv7_gain, proj_gain=proj_gain, proj_weight=proj_weight, proj_bias=proj_bias, pos_weight=pos_weight, pos_bias=pos_bias, out_gain=out_gain, out_bias=out_bias, lengths=lengths, crops=crops)


epsilon = 1e-05

def layer_norm(values, gain):
    centre = lax.optimization_barrier(jnp.mean(values, -1, keepdims=True))
    centred = values - centre
    spread = lax.optimization_barrier(jnp.mean(centred * centred, -1, keepdims=True))
    return centred * lax.rsqrt(spread + epsilon) * gain

def conv_layer(padded, out_rows, weight, gain, kernel):
    pieces = [padded[start:start + 2 * out_rows:2] for start in range(kernel)]
    joined = jnp.concatenate(pieces, 1)
    product = jnp.dot(joined, weight, preferred_element_type=jnp.float32)
    return jax.nn.gelu(layer_norm(product, gain), approximate=False).astype(jnp.bfloat16)

def project(frames, gain, weight, bias):
    normed = layer_norm(frames.astype(jnp.float32), gain).astype(jnp.bfloat16)
    return (jnp.dot(normed, weight, preferred_element_type=jnp.float32) + bias).astype(jnp.bfloat16)

def reference(features, conv5_weight, conv6_weight, conv7_weight, conv5_gain, conv6_gain, conv7_gain, proj_gain, proj_weight, proj_bias, pos_weight, pos_bias, out_gain, out_bias, lengths, crops):

    def one_record(packed):
        signal, length, crop = packed
        extra = jnp.zeros((1, signal.shape[1]), signal.dtype)
        hidden = conv_layer(jnp.concatenate([signal, extra], 0), signal.shape[0] // 2, conv5_weight, conv5_gain, 3)
        hidden = conv_layer(hidden, hidden.shape[0] // 2, conv6_weight, conv6_gain, 2)
        hidden = conv_layer(hidden, hidden.shape[0] // 2, conv7_weight, conv7_gain, 2)
        projected = project(hidden, proj_gain, proj_weight, proj_bias)
        padded = jnp.concatenate([projected, projected], 0)
        moved = lax.dynamic_slice_in_dim(padded, crop.astype(jnp.int32), FRAMES, 0)
        source = (jnp.arange(FRAMES, dtype=jnp.int32) + crop.astype(jnp.int32)) % FRAMES
        valid = (source < length)[:, None]
        return jnp.where(valid, moved, jnp.zeros_like(moved))
    cropped = lax.map(one_record, (features, lengths, crops))
    inputs = cropped.astype(jnp.float32)
    kernel = pos_weight.astype(jnp.float32).transpose(1, 2, 0, 3).reshape(KPOS, GW, D)
    conv = lax.conv_general_dilated(inputs, kernel, (1,), [(KPOS // 2, KPOS // 2 - 1)], dimension_numbers=('NWC', 'WIO', 'NWC'), feature_group_count=GROUPS, precision=lax.Precision.HIGHEST)
    summed = inputs + jax.nn.gelu(conv + pos_bias, approximate=False)
    return (layer_norm(summed, out_gain) + out_bias).astype(jnp.bfloat16)
```

```python
import functools

import jax
import jax.numpy as jnp
from jax import lax
from jax.experimental import pallas as pl
from jax.experimental.pallas import tpu as pltpu
from jax.sharding import PartitionSpec as P

epsilon = 1e-05
f32 = jnp.float32
bf16 = jnp.bfloat16
TUP = 3
LANES = 256
MIB = 1 << 20


def gelu(x):
    return 0.5 * x * (1.0 + lax.erf(x * 0.7071067811865476))


def layer_norm(values, gain):
    centre = jnp.mean(values, -1, keepdims=True)
    centred = values - centre
    spread = jnp.mean(centred * centred, -1, keepdims=True)
    return centred * lax.rsqrt(spread + epsilon) * gain


def dot(a, b):
    return jnp.dot(a, b, preferred_element_type=f32)


def put(columns, first, value, stride=None):
    for c in range(columns.shape[0]):
        at = pl.ds(first, value.shape[0], stride=stride)
        columns[c, at, :] = value[:, c * 128 : (c + 1) * 128]


def take(columns, first, count, stride):
    return jnp.concatenate(
        [columns[c, pl.ds(first, count, stride=stride), :] for c in range(columns.shape[0])], 1
    )


def front_kernel(has_prev, *refs):
    if has_prev:
        prev_ref, refs = refs[0], refs[1:]
    feat, nxt, w5, w6, w7, g5, g6, g7, gp, out, rows = refs
    n = feat.shape[1]
    f = n // 8
    put(rows, 0, feat[0].astype(f32))
    put(rows, n, nxt[0, 0:1, :].astype(f32))
    x = [take(rows, k, f, 8).astype(bf16) for k in range(9)]
    joined = jnp.concatenate(
        [jnp.concatenate(x[k : k + 7 : 2], 0) for k in range(3)], 1
    )
    h = gelu(layer_norm(dot(joined, w5[...]), g5[...])).astype(bf16)
    for weight, gain in ((w6, g6), (w7, g7)):
        count = h.shape[0] // f
        joined = jnp.concatenate(
            [
                jnp.concatenate([h[i * f : (i + 1) * f] for i in range(k, count, 2)], 0)
                for k in range(2)
            ],
            1,
        )
        h = gelu(layer_norm(dot(joined, weight[...]), gain[...])).astype(bf16)
    normed = layer_norm(h.astype(f32), gp[...]).astype(bf16)
    if has_prev:
        out[0:f, :] = prev_ref[...]
        out[f : 2 * f, :] = normed
    else:
        out[...] = normed


def front(half, prev, features, nxt, nxt_spec, weights, gains):
    rows, width = features.shape[1] // 2, features.shape[2]
    frames = rows // 8
    whole = lambda a: pl.BlockSpec(a.shape, lambda i: (0,) * a.ndim)
    args = ([prev] if half else []) + [features, nxt, *weights, *gains]
    specs = ([whole(prev)] if half else []) + [
        pl.BlockSpec((1, rows, width), lambda i: (0, half, 0)),
        nxt_spec,
        *[whole(w) for w in weights],
        *[whole(g) for g in gains],
    ]
    out_shape = (2 * frames if half else frames, width)
    flops = sum(2 * w.shape[0] * w.shape[1] * frames * m for w, m in zip(weights, (4, 2, 1)))
    return pl.pallas_call(
        functools.partial(front_kernel, bool(half)),
        grid=(1,),
        in_specs=specs,
        out_specs=pl.BlockSpec(out_shape, lambda i: (0, 0)),
        out_shape=jax.ShapeDtypeStruct(out_shape, bf16),
        scratch_shapes=[pltpu.VMEM((width // 128, rows + 8, 128), f32)],
        compiler_params=pltpu.CompilerParams(vmem_limit_bytes=40 * MIB),
        cost_estimate=pl.CostEstimate(
            flops=4 * flops, transcendentals=0, bytes_accessed=8 * MIB
        ),
        name="front_half%d" % half,
    )(*args)


def project_kernel(n_dest, groups, tuples, half_kernel, scal, b0, b1, b2, w, bias, *rest):
    outs, rows = rest[:n_dest], rest[n_dest]
    frames = b0.shape[0]
    rem, crop, length, first, total, me = [scal[i] for i in range(6)]
    rows[:, 0:8, :] = jnp.zeros((rows.shape[0], 8, 128), f32)
    for i, b in enumerate((b0, b1, b2)):
        put(rows, 8 + i * frames, b[...].astype(f32))
    rows[:, 8 + 3 * frames :, :] = jnp.zeros((rows.shape[0], 16, 128), f32)
    lead = TUP - 1
    parts = []
    for a in range(TUP):
        picked = take(rows, 8 - lead + a + rem, tuples, TUP).astype(bf16)
        value = dot(picked, w[...]) + bias[...]
        x = TUP * lax.broadcasted_iota(jnp.int32, (tuples, 1), 0) + a
        j = first - half_kernel - lead + x
        s = j + crop
        s = jnp.where(s >= total, s - total, s)
        good = (x >= lead) & (x < lead + frames + 2 * half_kernel) & (j >= 0) & (j < total)
        good = good & (s < length)
        parts.append(jnp.where(good, value, 0.0).astype(bf16))
    width = w.shape[1] // n_dest
    gw = width // groups
    pad = jnp.zeros((tuples, LANES - TUP * gw), bf16)
    for dest in range(n_dest):
        pieces = []
        for g in range(groups):
            at = dest * width + g * gw
            pieces.append(
                jnp.concatenate([p[:, at : at + gw] for p in parts] + [pad], 1)
            )
        for d in range(n_dest):

            @pl.when(me == dest ^ d)
            def _(d=d, pieces=pieces):
                for g in range(groups):
                    outs[d][g] = pieces[g]


def project(blocks, w, bias, scal, n_dest, groups, tuples, half_kernel):
    frames, width = blocks[0].shape
    whole = lambda a: pl.BlockSpec(a.shape, lambda i, s: (0,) * a.ndim)
    shape = (groups, tuples, LANES)
    return pl.pallas_call(
        functools.partial(project_kernel, n_dest, groups, tuples, half_kernel),
        grid_spec=pltpu.PrefetchScalarGridSpec(
            num_scalar_prefetch=1,
            grid=(1,),
            in_specs=[*[whole(b) for b in blocks], whole(w), whole(bias)],
            out_specs=[pl.BlockSpec(shape, lambda i, s: (0, 0, 0))] * n_dest,
            scratch_shapes=[pltpu.VMEM((width // 128, 3 * frames + 24, 128), f32)],
        ),
        out_shape=[jax.ShapeDtypeStruct(shape, bf16)] * n_dest,
        compiler_params=pltpu.CompilerParams(vmem_limit_bytes=40 * MIB),
        name="project_window",
    )(scal, *blocks, w, bias)


def expand_kernel(tiles, gw, w, out):
    taps = w.shape[1]
    n = TUP * gw
    flat = w[0].reshape(taps * gw, gw)
    zero = jnp.zeros((gw, gw), bf16)
    for j in range(tiles):
        cols = []
        for b in range(TUP):
            rows = []
            for a in range(TUP):
                k = TUP * j + a - b - (TUP - 1)
                rows.append(flat[k * gw : (k + 1) * gw] if 0 <= k < taps else zero)
            cols.append(jnp.concatenate(rows, 0))
        cols.append(jnp.zeros((n, LANES - n), bf16))
        out[0, j, 0:n, :] = jnp.concatenate(cols, 1)
        out[0, j, n:LANES, :] = jnp.zeros((LANES - n, LANES), bf16)


def expand(pos_weight, tiles):
    groups, taps, gw, _ = pos_weight.shape
    return pl.pallas_call(
        functools.partial(expand_kernel, tiles, gw),
        grid=(groups,),
        in_specs=[pl.BlockSpec((1, taps, gw, gw), lambda g: (g, 0, 0, 0))],
        out_specs=pl.BlockSpec((1, tiles, LANES, LANES), lambda g: (g, 0, 0, 0)),
        out_shape=jax.ShapeDtypeStruct((groups, tiles, LANES, LANES), bf16),
        compiler_params=pltpu.CompilerParams(vmem_limit_bytes=40 * MIB),
        cost_estimate=pl.CostEstimate(
            flops=0, transcendentals=0, bytes_accessed=groups * tiles * LANES * LANES * 3
        ),
        name="expand_taps",
    )(pos_weight)


def on_device_conv(parts, table, bias, scal, n_rec, frames, tiles, gw, centre):
    groups = table.shape[0]
    phases = 16 // n_rec
    step = -(-(frames // phases) // TUP)
    depth = step + tiles
    tuples = parts[0].shape[1]
    lanes = 16
    return pl.pallas_call(
        functools.partial(conv_kernel, n_rec, phases, step, tiles, gw, frames, centre),
        grid_spec=pltpu.PrefetchScalarGridSpec(
            num_scalar_prefetch=1,
            grid=(groups,),
            in_specs=[
                *[pl.BlockSpec((1, tuples, LANES), lambda g, s: (g, 0, 0))] * n_rec,
                pl.BlockSpec((1, tiles, LANES, LANES), lambda g, s: (g, 0, 0, 0)),
                pl.BlockSpec((1, 1, LANES), lambda g, s: (g, 0, 0)),
            ],
            out_specs=pl.BlockSpec((n_rec, frames, groups * gw), lambda g, s: (0, 0, 0)),
            scratch_shapes=[
                pltpu.VMEM((tuples, LANES), f32),
                pltpu.VMEM((LANES // 128, depth * lanes, 128), f32),
                pltpu.VMEM((depth * lanes, LANES), bf16),
                pltpu.VMEM((groups, LANES // 128, step * lanes, 128), f32),
                pltpu.VMEM((-(-groups * gw // 128), n_rec * frames, 128), f32),
            ],
        ),
        out_shape=jax.ShapeDtypeStruct((n_rec, frames, groups * gw), f32),
        compiler_params=pltpu.CompilerParams(vmem_limit_bytes=48 * MIB),
        name="pos_conv",
    )(scal, *parts, table, bias)


def conv_kernel(n_rec, phases, step, tiles, gw, frames, centre, scal, *refs):
    parts, (table, bias, summed, wide, x_f32, x_b, s_f32, plain) = refs[:n_rec], refs[n_rec:]
    me = scal[0]
    lanes = n_rec * phases
    depth = step + tiles
    m = step * lanes
    g = pl.program_id(0)
    for d in range(n_rec):
        wide[...] = parts[d][0].astype(f32)
        rec = me ^ d
        for p in range(phases):
            put(x_f32, rec * phases + p, wide[p * step : p * step + depth, :], lanes)
    for c in range(LANES // 128):
        x_b[:, c * 128 : (c + 1) * 128] = x_f32[c].astype(bf16)
    total = jnp.zeros((m, LANES), f32)
    for j in range(tiles):
        total = total + dot(x_b[lanes * j : lanes * j + m, :], table[0, j])
    own = x_b[lanes * centre : lanes * centre + m, :].astype(f32)
    put(s_f32.at[g], 0, own + gelu(total + bias[0]))

    @pl.when(g == pl.num_programs(0) - 1)
    def _():
        groups = s_f32.shape[0]
        share = TUP * step
        for r in range(n_rec):
            for p in range(phases):
                rows = [take(s_f32.at[i], r * phases + p, step, lanes) for i in range(groups)]
                for b in range(TUP):
                    count = -(-(min(share, frames - p * share) - b) // TUP)
                    line = jnp.concatenate([v[:, b * gw : (b + 1) * gw] for v in rows], 1)
                    gap = plain.shape[0] * 128 - groups * gw
                    line = jnp.concatenate([line, jnp.zeros((step, gap), f32)], 1)
                    put(plain, r * frames + p * share + b, line[0:count], TUP)
        for r in range(n_rec):
            for c in range(plain.shape[0]):
                end = min(groups * gw, (c + 1) * 128)
                summed[r, :, c * 128 : end] = plain[c, r * frames : (r + 1) * frames, 0 : end - c * 128]


def on_device(
    features,
    conv5_weight,
    conv6_weight,
    conv7_weight,
    conv5_gain,
    conv6_gain,
    conv7_gain,
    proj_gain,
    proj_weight,
    proj_bias,
    pos_weight,
    pos_bias,
    out_gain,
    out_bias,
    lengths,
    crops,
):
    tm, grp = lax.axis_size("tm"), lax.axis_size("grp")
    groups, taps, gw, _ = pos_weight.shape
    half_kernel = taps // 2
    frames = features.shape[1] // 8
    total = frames * tm
    crop, length = crops[0], lengths[0]

    back = [(i + 1, i) for i in range(tm - 1)]
    edge = lax.ppermute(features[:, :1, :], "tm", back)
    weights = (conv5_weight, conv6_weight, conv7_weight)
    gains = [g[None] for g in (conv5_gain, conv6_gain, conv7_gain, proj_gain)]
    width = features.shape[2]
    inner = pl.BlockSpec((1, 16, width), lambda i: (0, 4 * frames // 16, 0))
    first_half = front(0, None, features, features, inner, weights, gains)
    outer = pl.BlockSpec((1, 1, width), lambda i: (0, 0, 0))
    normed = front(1, first_half, features, edge, outer, weights, gains)

    start = crop - half_kernel
    whole_blocks = jnp.floor_divide(start, frames)
    rem = start - whole_blocks * frames

    def from_block(distance):
        distance %= tm
        if distance == 0:
            return lambda v: v
        route = [((i + distance) % tm, i) for i in range(tm)]
        return lambda v: lax.ppermute(v, "tm", route)

    def branch(first):
        return lambda v: tuple(from_block(first + i)(v) for i in range(3))

    lowest = -(-half_kernel // frames)
    most = tm // 2
    blocks = lax.switch(
        whole_blocks + lowest, [branch(b) for b in range(-lowest, most)], normed
    )

    n_rec = grp
    phases = 16 // n_rec
    step = -(-(frames // phases) // TUP)
    tiles = -(-(taps + 2 * (TUP - 1)) // TUP)
    tuples = -(-(step * phases + tiles) // 8) * 8
    me = lax.axis_index("grp")
    scal = jnp.stack(
        [rem, crop, length, lax.axis_index("tm") * frames, jnp.int32(total), me]
    ).astype(jnp.int32)
    parts = project(
        blocks, proj_weight, proj_bias[None], scal, n_rec, groups, tuples, half_kernel
    )
    parts = [
        p if d == 0 else lax.ppermute(p, "grp", [(i ^ d, i) for i in range(grp)])
        for d, p in enumerate(parts)
    ]
    table = expand(pos_weight, tiles)
    lane_bias = jnp.pad(
        jnp.tile(pos_bias.reshape(groups, 1, gw), (1, 1, TUP)),
        ((0, 0), (0, 0), (0, LANES - TUP * gw)),
    )
    centre = (half_kernel + TUP - 1) // TUP
    summed = on_device_conv(
        parts, table, lane_bias, me[None].astype(jnp.int32), n_rec, frames, tiles, gw, centre
    )
    own = jnp.concatenate([jnp.sum(summed, -1), jnp.sum(summed * summed, -1)], 0)
    totals = own
    for d in range(1, grp):
        totals = totals + lax.ppermute(own, "grp", [(i ^ d, i) for i in range(grp)])
    channels = proj_weight.shape[1]
    centre_of = totals[:n_rec] / channels
    spread = totals[n_rec:] / channels - centre_of * centre_of
    scaled = (summed - centre_of[..., None]) * lax.rsqrt(spread + epsilon)[
        ..., None
    ] * out_gain + out_bias
    return scaled.astype(bf16)


def solution(mesh):
    return jax.shard_map(
        on_device,
        mesh=mesh,
        in_specs=(
            P("grp", "tm", None),
            P(),
            P(),
            P(),
            P(),
            P(),
            P(),
            P(),
            P(),
            P(),
            P("grp", None, None, None),
            P("grp"),
            P("grp"),
            P("grp"),
            P("grp"),
            P("grp"),
        ),
        out_specs=P(None, "tm", "grp"),
        check_vma=False,
    )
```

```python
import functools

import jax
import jax.numpy as jnp
from jax import lax
from jax.experimental import pallas as pl
from jax.experimental.pallas import tpu as pltpu
from jax.sharding import PartitionSpec as P

epsilon = 1e-05
f32 = jnp.float32
bf16 = jnp.bfloat16
TUP = 3
LANES = 256
MIB = 1 << 20


def gelu(x):
    return 0.5 * x * (1.0 + lax.erf(x * 0.7071067811865476))


def layer_norm(values, gain):
    centre = jnp.mean(values, -1, keepdims=True)
    centred = values - centre
    spread = jnp.mean(centred * centred, -1, keepdims=True)
    return centred * lax.rsqrt(spread + epsilon) * gain


def dot(a, b):
    return jnp.dot(a, b, preferred_element_type=f32)


def put(columns, first, value, stride=None):
    for c in range(columns.shape[0]):
        at = pl.ds(first, value.shape[0], stride=stride)
        columns[c, at, :] = value[:, c * 128 : (c + 1) * 128]


def take(columns, first, count, stride):
    return jnp.concatenate(
        [columns[c, pl.ds(first, count, stride=stride), :] for c in range(columns.shape[0])], 1
    )


def front_kernel(half, *refs):
    if half:
        prev_ref, refs = refs[0], refs[1:]
    feat, nxt, w5, w6, w7, *gains, out, rows, block, edge, v5, v6, v7, sems = refs
    gains = [g[...].reshape(1, -1) for g in gains]
    n = block.shape[0]
    f = n // 8
    copies = [
        pltpu.make_async_copy(feat.at[0, pl.ds(half * n, n), :], block, sems.at[0]),
        pltpu.make_async_copy(
            nxt.at[0] if half else nxt.at[0, pl.ds(n, edge.shape[0]), :], edge, sems.at[1]
        ),
        pltpu.make_async_copy(w5, v5, sems.at[2]),
        pltpu.make_async_copy(w6, v6, sems.at[3]),
        pltpu.make_async_copy(w7, v7, sems.at[4]),
    ]
    for copy in copies:
        copy.start()
    copies[0].wait()
    put(rows, 0, block[...].astype(f32))
    copies[1].wait()
    put(rows, n, edge[0:1, :].astype(f32))
    x = [take(rows, k, f, 8).astype(bf16) for k in range(9)]
    joined = jnp.concatenate(
        [jnp.concatenate(x[k : k + 7 : 2], 0) for k in range(3)], 1
    )
    copies[2].wait()
    h = gelu(layer_norm(dot(joined, v5[...]), gains[0])).astype(bf16)
    for layer, weight in ((1, v6), (2, v7)):
        count = h.shape[0] // f
        joined = jnp.concatenate(
            [
                jnp.concatenate([h[i * f : (i + 1) * f] for i in range(k, count, 2)], 0)
                for k in range(2)
            ],
            1,
        )
        copies[2 + layer].wait()
        h = gelu(layer_norm(dot(joined, weight[...]), gains[layer])).astype(bf16)
    normed = layer_norm(h.astype(f32), gains[3]).astype(bf16)
    if half:
        out[0:f, :] = prev_ref[...]
        out[f : 2 * f, :] = normed
    else:
        out[...] = normed


def front(half, prev, features, nxt, weights, gains):
    rows, width = features.shape[1] // 2, features.shape[2]
    frames = rows // 8
    whole = lambda a: pl.BlockSpec(a.shape, lambda i: (0,) * a.ndim)
    far = pl.BlockSpec(memory_space=pltpu.MemorySpace.HBM)
    args = ([prev] if half else []) + [features, nxt, *weights, *gains]
    specs = ([whole(prev)] if half else []) + [far] * 5 + [whole(g) for g in gains]
    out_shape = (2 * frames if half else frames, width)
    flops = sum(2 * w.shape[0] * w.shape[1] * frames * m for w, m in zip(weights, (4, 2, 1)))
    return pl.pallas_call(
        functools.partial(front_kernel, half),
        grid=(1,),
        in_specs=specs,
        out_specs=pl.BlockSpec(out_shape, lambda i: (0, 0)),
        out_shape=jax.ShapeDtypeStruct(out_shape, bf16),
        scratch_shapes=[
            pltpu.VMEM((width // 128, rows + 8, 128), f32),
            pltpu.VMEM((rows, width), bf16),
            pltpu.VMEM((1 if half else 16, width), bf16),
            *[pltpu.VMEM(w.shape, bf16) for w in weights],
            pltpu.SemaphoreType.DMA((5,)),
        ],
        cost_estimate=pl.CostEstimate(
            flops=4 * flops, transcendentals=0, bytes_accessed=8 * MIB
        ),
        name="front_half%d" % half,
    )(*args)


def project_kernel(n_dest, groups, tuples, half_kernel, crops, lengths, b0, b1, b2, w, bias, *rest):
    outs, rows = rest[:n_dest], rest[n_dest]
    frames = b0.shape[0]
    crop, length = crops[0], lengths[0]
    rem = lax.rem(crop - half_kernel + 2 * half_kernel * frames, frames)
    first, total = lax.axis_index("tm") * frames, lax.axis_size("tm") * frames
    me = lax.axis_index("grp")
    rows[:, 0:8, :] = jnp.zeros((rows.shape[0], 8, 128), f32)
    for i, b in enumerate((b0, b1, b2)):
        put(rows, 8 + i * frames, b[...].astype(f32))
    rows[:, 8 + 3 * frames :, :] = jnp.zeros((rows.shape[0], 16, 128), f32)
    lead = TUP - 1
    parts = []
    for a in range(TUP):
        picked = take(rows, 8 - lead + a + rem, tuples, TUP).astype(bf16)
        value = dot(picked, w[...]) + bias[...].reshape(1, -1)
        x = TUP * lax.broadcasted_iota(jnp.int32, (tuples, 1), 0) + a
        j = first - half_kernel - lead + x
        s = j + crop
        s = jnp.where(s >= total, s - total, s)
        good = (x >= lead) & (x < lead + frames + 2 * half_kernel) & (j >= 0) & (j < total)
        good = good & (s < length)
        parts.append(jnp.where(good, value, 0.0).astype(bf16))
    width = w.shape[1] // n_dest
    gw = width // groups
    pad = jnp.zeros((tuples, LANES - TUP * gw), bf16)
    for dest in range(n_dest):
        pieces = []
        for g in range(groups):
            at = dest * width + g * gw
            pieces.append(
                jnp.concatenate([p[:, at : at + gw] for p in parts] + [pad], 1)
            )
        for d in range(n_dest):

            @pl.when(me == dest ^ d)
            def _(d=d, pieces=pieces):
                for g in range(groups):
                    outs[d][g] = pieces[g]


def project(blocks, w, bias, crops, lengths, n_dest, groups, tuples, half_kernel):
    frames, width = blocks[0].shape
    whole = lambda a: pl.BlockSpec(a.shape, lambda i, *s: (0,) * a.ndim)
    shape = (groups, tuples, LANES)
    return pl.pallas_call(
        functools.partial(project_kernel, n_dest, groups, tuples, half_kernel),
        grid_spec=pltpu.PrefetchScalarGridSpec(
            num_scalar_prefetch=2,
            grid=(1,),
            in_specs=[*[whole(b) for b in blocks], whole(w), whole(bias)],
            out_specs=[pl.BlockSpec(shape, lambda i, *s: (0, 0, 0))] * n_dest,
            scratch_shapes=[pltpu.VMEM((width // 128, 3 * frames + 24, 128), f32)],
        ),
        out_shape=[jax.ShapeDtypeStruct(shape, bf16)] * n_dest,
        compiler_params=pltpu.CompilerParams(vmem_limit_bytes=40 * MIB),
        name="project_window",
    )(crops, lengths, *blocks, w, bias)


def by_tap_kernel(w, out, wide):
    gw, taps = w.shape[1], w.shape[3]
    none = jnp.zeros((128 - gw, taps), f32)

    def one(i, carry):
        put(wide, i, jnp.concatenate([w[0, i].astype(f32), none], 0).T, gw)
        return carry

    lax.fori_loop(0, gw, one, 0, unroll=20)
    step = 4 * gw
    for first in range(0, taps * gw, step):
        out[0, first : first + step, :] = wide[0, first : first + step, :].astype(bf16)


def by_tap(by_channel):
    groups, gw, _, taps = by_channel.shape
    return pl.pallas_call(
        by_tap_kernel,
        grid=(groups,),
        in_specs=[pl.BlockSpec((1, gw, gw, taps), lambda g: (g, 0, 0, 0))],
        out_specs=pl.BlockSpec((1, taps * gw, 128), lambda g: (g, 0, 0)),
        out_shape=jax.ShapeDtypeStruct((groups, taps * gw, 128), bf16),
        scratch_shapes=[pltpu.VMEM((1, taps * gw, 128), f32)],
        cost_estimate=pl.CostEstimate(
            flops=0, transcendentals=0, bytes_accessed=groups * taps * gw * 128 * 8
        ),
        name="by_tap",
    )(by_channel)


def pos_conv_kernel(n_rec, phases, step, tiles, gw, frames, centre, *refs):
    parts, (flat, bias, summed, sums, wide, x_f32, x_b, s_f32, plain) = refs[:n_rec], refs[n_rec:]
    me = lax.axis_index("grp")
    taps = flat.shape[1] // gw
    groups = s_f32.shape[0]
    lanes = n_rec * phases
    depth = step + tiles
    m = step * lanes
    n = TUP * gw
    g = pl.program_id(0)
    for d in range(n_rec):
        wide[...] = parts[d][0].astype(f32)
        rec = me ^ d
        for p in range(phases):
            put(x_f32, rec * phases + p, wide[p * step : p * step + depth, :], lanes)
    for c in range(LANES // 128):
        x_b[:, c * 128 : (c + 1) * 128] = x_f32[c].astype(bf16)
    total = jnp.zeros((m, LANES), f32)
    zero = jnp.zeros((gw, gw), bf16)
    for j in range(tiles):
        cols = []
        for b in range(TUP):
            taps_of = [TUP * j + a - b - (TUP - 1) for a in range(TUP)]
            cols.append(
                jnp.concatenate(
                    [
                        flat[0, k * gw : (k + 1) * gw, 0:gw] if 0 <= k < taps else zero
                        for k in taps_of
                    ],
                    0,
                )
            )
        cols.append(jnp.zeros((n, LANES - n), bf16))
        total = total + dot(x_b[lanes * j : lanes * j + m, 0:n], jnp.concatenate(cols, 1))
    own = x_b[lanes * centre : lanes * centre + m, :].astype(f32)
    rows = [bias[...].reshape(1, -1)[:, i * gw : (i + 1) * gw] for i in range(groups)]
    gap = jnp.zeros((1, LANES - n), f32)
    shift = jnp.zeros((1, LANES), f32)
    for i in range(groups):
        shift = jnp.where(g == i, jnp.concatenate([rows[i]] * TUP + [gap], 1), shift)
    put(s_f32.at[g], 0, own + gelu(total + shift))

    @pl.when(g == groups - 1)
    def _():
        share = TUP * step
        for r in range(n_rec):
            for p in range(phases):
                rows = [take(s_f32.at[i], r * phases + p, step, lanes) for i in range(groups)]
                for b in range(TUP):
                    count = -(-(min(share, frames - p * share) - b) // TUP)
                    line = jnp.concatenate([v[:, b * gw : (b + 1) * gw] for v in rows], 1)
                    gap = plain.shape[0] * 128 - groups * gw
                    line = jnp.concatenate([line, jnp.zeros((step, gap), f32)], 1)
                    put(plain, r * frames + p * share + b, line[0:count], TUP)
        for r in range(n_rec):
            first = jnp.zeros((1, frames), f32)
            second = jnp.zeros((1, frames), f32)
            for c in range(plain.shape[0]):
                end = min(groups * gw, (c + 1) * 128)
                turned = plain[c, r * frames : (r + 1) * frames, :].T[0 : end - c * 128]
                summed[r, c * 128 : end, :] = turned
                first = first + jnp.sum(turned, 0, keepdims=True)
                second = second + jnp.sum(turned * turned, 0, keepdims=True)
            sums[r : r + 1, :] = first
            sums[n_rec + r : n_rec + r + 1, :] = second


def pos_conv(parts, flat, bias, n_rec, frames, tiles, gw, centre):
    groups = flat.shape[0]
    phases = 16 // n_rec
    step = -(-(frames // phases) // TUP)
    depth = step + tiles
    tuples = parts[0].shape[1]
    lanes = 16
    width = groups * gw
    return pl.pallas_call(
        functools.partial(pos_conv_kernel, n_rec, phases, step, tiles, gw, frames, centre),
        grid=(groups,),
        in_specs=[
            *[pl.BlockSpec((1, tuples, LANES), lambda g: (g, 0, 0))] * n_rec,
            pl.BlockSpec((1, flat.shape[1], 128), lambda g: (g, 0, 0)),
            pl.BlockSpec(bias.shape, lambda g: (0,)),
        ],
        out_specs=[
            pl.BlockSpec((n_rec, width, frames), lambda g: (0, 0, 0)),
            pl.BlockSpec((2 * n_rec, frames), lambda g: (0, 0)),
        ],
        scratch_shapes=[
            pltpu.VMEM((tuples, LANES), f32),
            pltpu.VMEM((LANES // 128, depth * lanes, 128), f32),
            pltpu.VMEM((depth * lanes, LANES), bf16),
            pltpu.VMEM((groups, LANES // 128, step * lanes, 128), f32),
            pltpu.VMEM((-(-width // 128), n_rec * frames, 128), f32),
        ],
        out_shape=[
            jax.ShapeDtypeStruct((n_rec, width, frames), f32),
            jax.ShapeDtypeStruct((2 * n_rec, frames), f32),
        ],
        compiler_params=pltpu.CompilerParams(vmem_limit_bytes=48 * MIB),
        name="pos_conv",
    )(*parts, flat, bias)


def on_device(
    features,
    conv5_weight,
    conv6_weight,
    conv7_weight,
    conv5_gain,
    conv6_gain,
    conv7_gain,
    proj_gain,
    proj_weight,
    proj_bias,
    pos_weight,
    pos_bias,
    out_gain,
    out_bias,
    lengths,
    crops,
):
    tm, grp = lax.axis_size("tm"), lax.axis_size("grp")
    groups, taps, gw, _ = pos_weight.shape
    half_kernel = taps // 2
    frames = features.shape[1] // 8
    crop = crops[0]

    back = [(i + 1, i) for i in range(tm - 1)]
    edge = lax.ppermute(features[:, :1, :], "tm", back)
    weights = (conv5_weight, conv6_weight, conv7_weight)
    gains = (conv5_gain, conv6_gain, conv7_gain, proj_gain)
    first_half = front(0, None, features, features, weights, gains)
    normed = front(1, first_half, features, edge, weights, gains)

    start = crop - half_kernel
    whole_blocks = jnp.floor_divide(start, frames)

    def from_block(distance):
        distance %= tm
        if distance == 0:
            return lambda v: v
        route = [((i + distance) % tm, i) for i in range(tm)]
        return lambda v: lax.ppermute(v, "tm", route)

    tiles = -(-(taps + 2 * (TUP - 1)) // TUP)

    def branch(first):
        return lambda v, w: (*[from_block(first + i)(v) for i in range(3)], by_tap(w))

    lowest = -(-half_kernel // frames)
    most = tm // 2
    *blocks, flat = lax.switch(
        whole_blocks + lowest,
        [branch(b) for b in range(-lowest, most)],
        normed,
        pos_weight.transpose(0, 2, 3, 1),
    )

    n_rec = grp
    phases = 16 // n_rec
    step = -(-(frames // phases) // TUP)
    tuples = -(-(step * phases + tiles) // 8) * 8
    parts = project(
        blocks, proj_weight, proj_bias, crops, lengths, n_rec, groups, tuples, half_kernel
    )
    parts = [
        p if d == 0 else lax.ppermute(p, "grp", [(i ^ d, i) for i in range(grp)])
        for d, p in enumerate(parts)
    ]
    centre = (half_kernel + TUP - 1) // TUP
    summed, own = pos_conv(parts, flat, pos_bias, n_rec, frames, tiles, gw, centre)
    totals = own
    for d in range(1, grp):
        totals = totals + lax.ppermute(own, "grp", [(i ^ d, i) for i in range(grp)])
    channels = proj_weight.shape[1]
    mean = totals[:n_rec] / channels
    spread = totals[n_rec:] / channels - mean * mean
    scaled = (summed - mean[:, None]) * lax.rsqrt(spread + epsilon)[:, None]
    scaled = scaled * out_gain[:, None] + out_bias[:, None]
    return scaled.astype(bf16).transpose(0, 2, 1)


def solution(mesh):
    return jax.shard_map(
        on_device,
        mesh=mesh,
        in_specs=(
            P("grp", "tm", None),
            P(),
            P(),
            P(),
            P(),
            P(),
            P(),
            P(),
            P(),
            P(),
            P("grp", None, None, None),
            P("grp"),
            P("grp"),
            P("grp"),
            P("grp"),
            P("grp"),
        ),
        out_specs=P(None, "tm", "grp"),
        check_vma=False,
    )
```

```python
import functools

import jax
import jax.numpy as jnp
from jax import lax
from jax.experimental import pallas as pl
from jax.experimental.pallas import tpu as pltpu
from jax.sharding import PartitionSpec as P

epsilon = 1e-05
f32 = jnp.float32
bf16 = jnp.bfloat16
TUP = 3
LANES = 256
MIB = 1 << 20


def gelu(x):
    return 0.5 * x * (1.0 + lax.erf(x * 0.7071067811865476))


def layer_norm(values, gain):
    centre = jnp.mean(values, -1, keepdims=True)
    centred = values - centre
    spread = jnp.mean(centred * centred, -1, keepdims=True)
    return centred * lax.rsqrt(spread + epsilon) * gain


def dot(a, b):
    return jnp.dot(a, b, preferred_element_type=f32)


def put(columns, first, value, stride=None):
    for c in range(columns.shape[0]):
        at = pl.ds(first, value.shape[0], stride=stride)
        columns[c, at, :] = value[:, c * 128 : (c + 1) * 128]


def take(columns, first, count, stride):
    return jnp.concatenate(
        [columns[c, pl.ds(first, count, stride=stride), :] for c in range(columns.shape[0])], 1
    )


def front_kernel(feat, nxt, w5, w6, w7, *refs):
    *gains, out, rows, block, v5, v6, v7, sems = refs
    gains = [g[...].reshape(1, -1) for g in gains]
    n = block.shape[0]
    f = n // 8
    sources = (feat.at[0], w5, w6, w7)
    copies = [
        pltpu.make_async_copy(source, target, sems.at[i])
        for i, (source, target) in enumerate(zip(sources, (block, v5, v6, v7)))
    ]
    for copy in copies:
        copy.start()
    copies[0].wait()
    put(rows, 0, block[...].astype(f32))
    put(rows, n, nxt[0].astype(f32))
    x = [take(rows, k, f, 8).astype(bf16) for k in range(9)]
    joined = jnp.concatenate(
        [jnp.concatenate(x[k : k + 7 : 2], 0) for k in range(3)], 1
    )
    copies[1].wait()
    h = gelu(layer_norm(dot(joined, v5[...]), gains[0])).astype(bf16)
    for layer, weight in ((1, v6), (2, v7)):
        count = h.shape[0] // f
        joined = jnp.concatenate(
            [
                jnp.concatenate([h[i * f : (i + 1) * f] for i in range(k, count, 2)], 0)
                for k in range(2)
            ],
            1,
        )
        copies[1 + layer].wait()
        h = gelu(layer_norm(dot(joined, weight[...]), gains[layer])).astype(bf16)
    out[...] = layer_norm(h.astype(f32), gains[3]).astype(bf16)


def front(features, nxt, weights, gains):
    rows, width = features.shape[1:]
    frames = rows // 8
    far = pl.BlockSpec(memory_space=pltpu.MemorySpace.HBM)
    flops = sum(2 * w.shape[0] * w.shape[1] * frames * m for w, m in zip(weights, (4, 2, 1)))
    return pl.pallas_call(
        front_kernel,
        grid=(1,),
        in_specs=[
            far,
            pl.BlockSpec(nxt.shape, lambda i: (0, 0, 0)),
            *[far] * 3,
            *[pl.BlockSpec(g.shape, lambda i: (0,)) for g in gains],
        ],
        out_specs=pl.BlockSpec((frames, width), lambda i: (0, 0)),
        out_shape=jax.ShapeDtypeStruct((frames, width), bf16),
        scratch_shapes=[
            pltpu.VMEM((width // 128, rows + 8, 128), f32),
            pltpu.VMEM((rows, width), bf16),
            *[pltpu.VMEM(w.shape, bf16) for w in weights],
            pltpu.SemaphoreType.DMA((4,)),
        ],
        cost_estimate=pl.CostEstimate(
            flops=4 * flops, transcendentals=0, bytes_accessed=8 * MIB
        ),
        name="front",
    )(features, nxt, *weights, *gains)


def project_kernel(n_dest, groups, tuples, half_kernel, crops, lengths, b0, b1, b2, w, bias, *rest):
    outs, rows = rest[:n_dest], rest[n_dest]
    frames = b0.shape[0]
    crop, length = crops[0], lengths[0]
    rem = lax.rem(crop - half_kernel + 2 * half_kernel * frames, frames)
    first, total = lax.axis_index("tm") * frames, lax.axis_size("tm") * frames
    me = lax.axis_index("grp")
    rows[:, 0:8, :] = jnp.zeros((rows.shape[0], 8, 128), f32)
    for i, b in enumerate((b0, b1, b2)):
        put(rows, 8 + i * frames, b[...].astype(f32))
    rows[:, 8 + 3 * frames :, :] = jnp.zeros((rows.shape[0], 16, 128), f32)
    lead = TUP - 1
    parts = []
    for a in range(TUP):
        picked = take(rows, 8 - lead + a + rem, tuples, TUP).astype(bf16)
        value = dot(picked, w[...]) + bias[...].reshape(1, -1)
        x = TUP * lax.broadcasted_iota(jnp.int32, (tuples, 1), 0) + a
        j = first - half_kernel - lead + x
        s = j + crop
        s = jnp.where(s >= total, s - total, s)
        good = (x >= lead) & (x < lead + frames + 2 * half_kernel) & (j >= 0) & (j < total)
        good = good & (s < length)
        parts.append(jnp.where(good, value, 0.0).astype(bf16))
    width = w.shape[1] // n_dest
    gw = width // groups
    pad = jnp.zeros((tuples, LANES - TUP * gw), bf16)
    for dest in range(n_dest):
        pieces = []
        for g in range(groups):
            at = dest * width + g * gw
            pieces.append(
                jnp.concatenate([p[:, at : at + gw] for p in parts] + [pad], 1)
            )
        for d in range(n_dest):

            @pl.when(me == dest ^ d)
            def _(d=d, pieces=pieces):
                for g in range(groups):
                    outs[d][g] = pieces[g]


def project(blocks, w, bias, crops, lengths, n_dest, groups, tuples, half_kernel):
    frames, width = blocks[0].shape
    whole = lambda a: pl.BlockSpec(a.shape, lambda i, *s: (0,) * a.ndim)
    shape = (groups, tuples, LANES)
    return pl.pallas_call(
        functools.partial(project_kernel, n_dest, groups, tuples, half_kernel),
        grid_spec=pltpu.PrefetchScalarGridSpec(
            num_scalar_prefetch=2,
            grid=(1,),
            in_specs=[*[whole(b) for b in blocks], whole(w), whole(bias)],
            out_specs=[pl.BlockSpec(shape, lambda i, *s: (0, 0, 0))] * n_dest,
            scratch_shapes=[pltpu.VMEM((width // 128, 3 * frames + 24, 128), f32)],
        ),
        out_shape=[jax.ShapeDtypeStruct(shape, bf16)] * n_dest,
        compiler_params=pltpu.CompilerParams(vmem_limit_bytes=40 * MIB),
        name="project_window",
    )(crops, lengths, *blocks, w, bias)


def by_tap_kernel(w, out, wide):
    gw, taps = w.shape[1], w.shape[3]
    none = jnp.zeros((128 - gw, taps), f32)

    def one(i, carry):
        put(wide, i, jnp.concatenate([w[0, i].astype(f32), none], 0).T, gw)
        return carry

    lax.fori_loop(0, gw, one, 0, unroll=20)
    step = 4 * gw
    for first in range(0, taps * gw, step):
        out[0, first : first + step, :] = wide[0, first : first + step, :].astype(bf16)


def by_tap(by_channel, first, count):
    _, gw, _, taps = by_channel.shape
    return pl.pallas_call(
        by_tap_kernel,
        grid=(count,),
        in_specs=[pl.BlockSpec((1, gw, gw, taps), lambda g: (g + first, 0, 0, 0))],
        out_specs=pl.BlockSpec((1, taps * gw, 128), lambda g: (g, 0, 0)),
        out_shape=jax.ShapeDtypeStruct((count, taps * gw, 128), bf16),
        scratch_shapes=[pltpu.VMEM((1, taps * gw, 128), f32)],
        cost_estimate=pl.CostEstimate(
            flops=0, transcendentals=0, bytes_accessed=count * taps * gw * 128 * 8
        ),
        name="by_tap_%d" % first,
    )(by_channel)


def pos_conv_kernel(n_rec, early, phases, step, tiles, gw, frames, centre, *refs):
    parts, refs = refs[:n_rec], refs[n_rec:]
    flat_a, flat_b, bias, summed, sums, flat, wide, x_f32, x_b, s_f32, plain, sems = refs
    me = lax.axis_index("grp")
    taps = flat_a.shape[1] // gw
    groups = s_f32.shape[0]
    lanes = n_rec * phases
    depth = step + tiles
    m = step * lanes
    n = TUP * gw
    g = pl.program_id(0)
    slot = lax.rem(g, 2)

    def fetch(i):
        source = flat_a.at[i] if i < early else flat_b.at[i - early]
        pltpu.make_async_copy(source, flat.at[i % 2], sems.at[i % 2]).start()

    @pl.when(g == 0)
    def _():
        for i in range(min(2, groups)):
            fetch(i)

    for d in range(n_rec):
        wide[0 : parts[d].shape[1], :] = parts[d][0].astype(f32)
        rec = me ^ d
        for p in range(phases):
            put(x_f32, rec * phases + p, wide[p * step : p * step + depth, :], lanes)
    for c in range(LANES // 128):
        x_b[:, c * 128 : (c + 1) * 128] = x_f32[c, 0 : depth * lanes, :].astype(bf16)
    zero = jnp.zeros((gw, gw), bf16)

    pltpu.make_async_copy(flat_a.at[0], flat.at[slot], sems.at[slot]).wait()
    total = jnp.zeros((m, LANES), f32)
    for j in range(tiles):
        cols = []
        for b in range(TUP):
            taps_of = [TUP * j + a - b - (TUP - 1) for a in range(TUP)]
            cols.append(
                jnp.concatenate(
                    [
                        flat[slot, k * gw : (k + 1) * gw, 0:gw] if 0 <= k < taps else zero
                        for k in taps_of
                    ],
                    0,
                )
            )
        cols.append(jnp.zeros((n, LANES - n), bf16))
        total = total + dot(x_b[lanes * j : lanes * j + m, 0:n], jnp.concatenate(cols, 1))
    for i in range(2, groups):

        @pl.when(g == i - 2)
        def _(i=i):
            fetch(i)

    own = x_b[lanes * centre : lanes * centre + m, :].astype(f32)
    rows = [bias[...].reshape(1, -1)[:, i * gw : (i + 1) * gw] for i in range(groups)]
    gap = jnp.zeros((1, LANES - n), f32)
    shift = jnp.zeros((1, LANES), f32)
    for i in range(groups):
        shift = jnp.where(g == i, jnp.concatenate([rows[i]] * TUP + [gap], 1), shift)
    put(s_f32.at[g], 0, own + gelu(total + shift))

    @pl.when(g == groups - 1)
    def _():
        share = TUP * step
        for r in range(n_rec):
            for p in range(phases):
                rows = [take(s_f32.at[i], r * phases + p, step, lanes) for i in range(groups)]
                for b in range(TUP):
                    count = -(-(min(share, frames - p * share) - b) // TUP)
                    line = jnp.concatenate([v[:, b * gw : (b + 1) * gw] for v in rows], 1)
                    gap = plain.shape[0] * 128 - groups * gw
                    line = jnp.concatenate([line, jnp.zeros((step, gap), f32)], 1)
                    put(plain, r * frames + p * share + b, line[0:count], TUP)
        for r in range(n_rec):
            first = jnp.zeros((1, frames), f32)
            second = jnp.zeros((1, frames), f32)
            for c in range(plain.shape[0]):
                end = min(groups * gw, (c + 1) * 128)
                turned = plain[c, r * frames : (r + 1) * frames, :].T[0 : end - c * 128]
                summed[r, c * 128 : end, :] = turned
                first = first + jnp.sum(turned, 0, keepdims=True)
                second = second + jnp.sum(turned * turned, 0, keepdims=True)
            sums[r : r + 1, :] = first
            sums[n_rec + r : n_rec + r + 1, :] = second


def pos_conv(parts, flat_a, flat_b, bias, n_rec, frames, tiles, gw, centre):
    early = flat_a.shape[0]
    groups = early + flat_b.shape[0]
    phases = 16 // n_rec
    step = -(-(frames // phases) // TUP)
    depth = step + tiles
    tuples = parts[0].shape[1]
    lanes = 16
    width = groups * gw
    return pl.pallas_call(
        functools.partial(pos_conv_kernel, n_rec, early, phases, step, tiles, gw, frames, centre),
        grid=(groups,),
        in_specs=[
            *[pl.BlockSpec((1, tuples, LANES), lambda g: (g, 0, 0))] * n_rec,
            *[pl.BlockSpec(memory_space=pltpu.MemorySpace.HBM)] * 2,
            pl.BlockSpec(bias.shape, lambda g: (0,)),
        ],
        out_specs=[
            pl.BlockSpec((n_rec, width, frames), lambda g: (0, 0, 0)),
            pl.BlockSpec((2 * n_rec, frames), lambda g: (0, 0)),
        ],
        scratch_shapes=[
            pltpu.VMEM((2, *flat_a.shape[1:]), bf16),
            pltpu.VMEM((tuples + 16, LANES), f32),
            pltpu.VMEM((LANES // 128, (depth + 9) * lanes, 128), f32),
            pltpu.VMEM((depth * lanes, LANES), bf16),
            pltpu.VMEM((groups, LANES // 128, (step + 9) * lanes, 128), f32),
            pltpu.VMEM((-(-width // 128), n_rec * frames + 64, 128), f32),
            pltpu.SemaphoreType.DMA((2,)),
        ],
        out_shape=[
            jax.ShapeDtypeStruct((n_rec, width, frames), f32),
            jax.ShapeDtypeStruct((2 * n_rec, frames), f32),
        ],
        compiler_params=pltpu.CompilerParams(vmem_limit_bytes=48 * MIB),
        name="pos_conv",
    )(*parts, flat_a, flat_b, bias)


def on_device(
    features,
    conv5_weight,
    conv6_weight,
    conv7_weight,
    conv5_gain,
    conv6_gain,
    conv7_gain,
    proj_gain,
    proj_weight,
    proj_bias,
    pos_weight,
    pos_bias,
    out_gain,
    out_bias,
    lengths,
    crops,
):
    tm, grp = lax.axis_size("tm"), lax.axis_size("grp")
    groups, taps, gw, _ = pos_weight.shape
    half_kernel = taps // 2
    frames = features.shape[1] // 8
    crop = crops[0]

    back = [(i + 1, i) for i in range(tm - 1)]
    edge = lax.ppermute(features[:, :1, :], "tm", back)
    weights = (conv5_weight, conv6_weight, conv7_weight)
    gains = (conv5_gain, conv6_gain, conv7_gain, proj_gain)
    by_channel = pos_weight.transpose(0, 2, 3, 1)
    early = groups // 2
    normed = front(features, edge, weights, gains)

    start = crop - half_kernel
    whole_blocks = jnp.floor_divide(start, frames)

    def from_block(distance):
        distance %= tm
        if distance == 0:
            return lambda v: v
        route = [((i + distance) % tm, i) for i in range(tm)]
        return lambda v: lax.ppermute(v, "tm", route)

    tiles = -(-(taps + 2 * (TUP - 1)) // TUP)

    def branch(first):
        return lambda v, w: (
            *[from_block(first + i)(v) for i in range(3)],
            by_tap(w, 0, early),
        )

    tiles = -(-(taps + 2 * (TUP - 1)) // TUP)
    lowest = -(-half_kernel // frames)
    most = tm // 2
    *blocks, flat_a = lax.switch(
        whole_blocks + lowest,
        [branch(b) for b in range(-lowest, most)],
        normed,
        by_channel,
    )

    n_rec = grp
    phases = 16 // n_rec
    step = -(-(frames // phases) // TUP)
    tuples = -(-(step * phases + tiles) // 8) * 8
    parts = project(
        blocks, proj_weight, proj_bias, crops, lengths, n_rec, groups, tuples, half_kernel
    )
    parts = [
        p if d == 0 else lax.ppermute(p, "grp", [(i ^ d, i) for i in range(grp)])
        for d, p in enumerate(parts)
    ]
    flat_b = by_tap(by_channel, early, groups - early)
    centre = (half_kernel + TUP - 1) // TUP
    summed, own = pos_conv(parts, flat_a, flat_b, pos_bias, n_rec, frames, tiles, gw, centre)
    totals = own
    for d in range(1, grp):
        totals = totals + lax.ppermute(own, "grp", [(i ^ d, i) for i in range(grp)])
    channels = proj_weight.shape[1]
    mean = totals[:n_rec] / channels
    spread = totals[n_rec:] / channels - mean * mean
    scaled = (summed - mean[:, None]) * lax.rsqrt(spread + epsilon)[:, None]
    scaled = scaled * out_gain[:, None] + out_bias[:, None]
    return scaled.astype(bf16).transpose(0, 2, 1)


def solution(mesh):
    return jax.shard_map(
        on_device,
        mesh=mesh,
        in_specs=(
            P("grp", "tm", None),
            P(),
            P(),
            P(),
            P(),
            P(),
            P(),
            P(),
            P(),
            P(),
            P("grp", None, None, None),
            P("grp"),
            P("grp"),
            P("grp"),
            P("grp"),
            P("grp"),
        ),
        out_specs=P(None, "tm", "grp"),
        check_vma=False,
    )
```

```python
import functools

import jax
import jax.numpy as jnp
from jax import lax
from jax.experimental import pallas as pl
from jax.experimental.pallas import tpu as pltpu
from jax.sharding import PartitionSpec as P

epsilon = 1e-05
f32 = jnp.float32
bf16 = jnp.bfloat16
TUP = 3
LANES = 256
MIB = 1 << 20


def gelu(x):
    return 0.5 * x * (1.0 + lax.erf(x * 0.7071067811865476))


def layer_norm(values, gain):
    centre = jnp.mean(values, -1, keepdims=True)
    centred = values - centre
    spread = jnp.mean(centred * centred, -1, keepdims=True)
    return centred * lax.rsqrt(spread + epsilon) * gain


def dot(a, b):
    return jnp.dot(a, b, preferred_element_type=f32)


def put(columns, first, value, stride=None):
    for c in range(columns.shape[0]):
        at = pl.ds(first, value.shape[0], stride=stride)
        columns[c, at, :] = value[:, c * 128 : (c + 1) * 128]


def take(columns, first, count, stride):
    return jnp.concatenate(
        [columns[c, pl.ds(first, count, stride=stride), :] for c in range(columns.shape[0])], 1
    )


def front_kernel(feat, nxt, w5, w6, w7, *refs):
    *gains, out, low, high, rows, block, v5, v6, v7, sems = refs
    gains = [g[...].reshape(1, -1) for g in gains]
    n = block.shape[0]
    f = n // 8
    sources = (feat.at[0], w5, w6, w7)
    copies = [
        pltpu.make_async_copy(source, target, sems.at[i])
        for i, (source, target) in enumerate(zip(sources, (block, v5, v6, v7)))
    ]
    for copy in copies:
        copy.start()
    copies[0].wait()
    put(rows, 0, block[...].astype(f32))
    put(rows, n, nxt[0].astype(f32))
    x = [take(rows, k, f, 8).astype(bf16) for k in range(9)]
    joined = jnp.concatenate(
        [jnp.concatenate(x[k : k + 7 : 2], 0) for k in range(3)], 1
    )
    copies[1].wait()
    h = gelu(layer_norm(dot(joined, v5[...]), gains[0])).astype(bf16)
    for layer, weight in ((1, v6), (2, v7)):
        count = h.shape[0] // f
        joined = jnp.concatenate(
            [
                jnp.concatenate([h[i * f : (i + 1) * f] for i in range(k, count, 2)], 0)
                for k in range(2)
            ],
            1,
        )
        copies[1 + layer].wait()
        h = gelu(layer_norm(dot(joined, weight[...]), gains[layer])).astype(bf16)
    normed = layer_norm(h.astype(f32), gains[3]).astype(bf16)
    out[...] = normed
    low[...] = normed[: f // 2]
    high[...] = normed[f // 2 :]


def front(features, nxt, weights, gains):
    rows, width = features.shape[1:]
    frames = rows // 8
    sizes = (frames, frames // 2, frames // 2)
    far = pl.BlockSpec(memory_space=pltpu.MemorySpace.HBM)
    flops = sum(2 * w.shape[0] * w.shape[1] * frames * m for w, m in zip(weights, (4, 2, 1)))
    return pl.pallas_call(
        front_kernel,
        grid=(1,),
        in_specs=[
            far,
            pl.BlockSpec(nxt.shape, lambda i: (0, 0, 0)),
            *[far] * 3,
            *[pl.BlockSpec(g.shape, lambda i: (0,)) for g in gains],
        ],
        out_specs=[pl.BlockSpec((n, width), lambda i: (0, 0)) for n in sizes],
        out_shape=[jax.ShapeDtypeStruct((n, width), bf16) for n in sizes],
        scratch_shapes=[
            pltpu.VMEM((width // 128, rows + 8, 128), f32),
            pltpu.VMEM((rows, width), bf16),
            *[pltpu.VMEM(w.shape, bf16) for w in weights],
            pltpu.SemaphoreType.DMA((4,)),
        ],
        cost_estimate=pl.CostEstimate(
            flops=4 * flops, transcendentals=0, bytes_accessed=8 * MIB
        ),
        name="front",
    )(features, nxt, *weights, *gains)


def project_kernel(n_dest, groups, tuples, half_kernel, crops, lengths, b0, b1, b2, w, bias, *rest):
    outs, rows = rest[:n_dest], rest[n_dest]
    frames = b0.shape[0]
    crop, length = crops[0], lengths[0]
    piece = b2.shape[0]
    rem = lax.rem(crop - half_kernel + 2 * half_kernel * frames, frames)
    odd = rem >= piece
    rem = jnp.where(odd, rem - piece, rem)
    first, total = lax.axis_index("tm") * frames, lax.axis_size("tm") * frames
    me = lax.axis_index("grp")
    rows[:, 0:8, :] = jnp.zeros((rows.shape[0], 8, 128), f32)
    at = pl.multiple_of(jnp.where(odd, 8 + piece, 8), 8)
    put(rows, at, b0[...].astype(f32))
    put(rows, pl.multiple_of(at + frames, 8), b1[...].astype(f32))
    put(rows, pl.multiple_of(jnp.where(odd, 8, 8 + 2 * frames), 8), b2[...].astype(f32))
    rows[:, 8 + 2 * frames + piece :, :] = jnp.zeros((rows.shape[0], 16, 128), f32)
    lead = TUP - 1
    parts = []
    for a in range(TUP):
        picked = take(rows, 8 - lead + a + rem, tuples, TUP).astype(bf16)
        value = dot(picked, w[...]) + bias[...].reshape(1, -1)
        x = TUP * lax.broadcasted_iota(jnp.int32, (tuples, 1), 0) + a
        j = first - half_kernel - lead + x
        s = j + crop
        s = jnp.where(s >= total, s - total, s)
        good = (x >= lead) & (x < lead + frames + 2 * half_kernel) & (j >= 0) & (j < total)
        good = good & (s < length)
        parts.append(jnp.where(good, value, 0.0).astype(bf16))
    width = w.shape[1] // n_dest
    gw = width // groups
    pad = jnp.zeros((tuples, LANES - TUP * gw), bf16)
    for dest in range(n_dest):
        pieces = []
        for g in range(groups):
            at = dest * width + g * gw
            pieces.append(
                jnp.concatenate([p[:, at : at + gw] for p in parts] + [pad], 1)
            )
        for d in range(n_dest):

            @pl.when(me == dest ^ d)
            def _(d=d, pieces=pieces):
                for g in range(groups):
                    outs[d][g] = pieces[g]


def project(blocks, w, bias, crops, lengths, n_dest, groups, tuples, half_kernel):
    frames, width = blocks[0].shape
    whole = lambda a: pl.BlockSpec(a.shape, lambda i, *s: (0,) * a.ndim)
    shape = (groups, tuples, LANES)
    return pl.pallas_call(
        functools.partial(project_kernel, n_dest, groups, tuples, half_kernel),
        grid_spec=pltpu.PrefetchScalarGridSpec(
            num_scalar_prefetch=2,
            grid=(1,),
            in_specs=[*[whole(b) for b in blocks], whole(w), whole(bias)],
            out_specs=[pl.BlockSpec(shape, lambda i, *s: (0, 0, 0))] * n_dest,
            scratch_shapes=[pltpu.VMEM((width // 128, 2 * frames + blocks[2].shape[0] + 24, 128), f32)],
        ),
        out_shape=[jax.ShapeDtypeStruct(shape, bf16)] * n_dest,
        compiler_params=pltpu.CompilerParams(vmem_limit_bytes=40 * MIB),
        name="project_window",
    )(crops, lengths, *blocks, w, bias)


def by_tap_kernel(w, out, wide):
    gw, taps = w.shape[1], w.shape[3]
    none = jnp.zeros((128 - gw, taps), f32)

    def one(i, carry):
        put(wide, i, jnp.concatenate([w[0, i].astype(f32), none], 0).T, gw)
        return carry

    lax.fori_loop(0, gw, one, 0, unroll=20)
    step = 4 * gw
    for first in range(0, taps * gw, step):
        out[0, first : first + step, :] = wide[0, first : first + step, :].astype(bf16)


def by_tap(by_channel, first, count):
    _, gw, _, taps = by_channel.shape
    return pl.pallas_call(
        by_tap_kernel,
        grid=(count,),
        in_specs=[pl.BlockSpec((1, gw, gw, taps), lambda g: (g + first, 0, 0, 0))],
        out_specs=pl.BlockSpec((1, taps * gw, 128), lambda g: (g, 0, 0)),
        out_shape=jax.ShapeDtypeStruct((count, taps * gw, 128), bf16),
        scratch_shapes=[pltpu.VMEM((1, taps * gw, 128), f32)],
        cost_estimate=pl.CostEstimate(
            flops=0, transcendentals=0, bytes_accessed=count * taps * gw * 128 * 8
        ),
        name="by_tap_%d" % first,
    )(by_channel)


def pos_conv_kernel(n_rec, early, phases, step, tiles, gw, frames, centre, *refs):
    parts, refs = refs[:n_rec], refs[n_rec:]
    flat_a, flat_b, bias, summed, sums, flat, wide, x_f32, x_b, s_f32, plain, sems = refs
    me = lax.axis_index("grp")
    taps = flat_a.shape[1] // gw
    groups = s_f32.shape[0]
    lanes = n_rec * phases
    depth = step + tiles
    m = step * lanes
    n = TUP * gw
    g = pl.program_id(0)
    slot = lax.rem(g, 2)

    def fetch(i):
        source = flat_a.at[i] if i < early else flat_b.at[i - early]
        pltpu.make_async_copy(source, flat.at[i % 2], sems.at[i % 2]).start()

    @pl.when(g == 0)
    def _():
        for i in range(min(2, groups)):
            fetch(i)

    for d in range(n_rec):
        wide[0 : parts[d].shape[1], :] = parts[d][0].astype(f32)
        rec = me ^ d
        for p in range(phases):
            put(x_f32, rec * phases + p, wide[p * step : p * step + depth, :], lanes)
    for c in range(LANES // 128):
        x_b[:, c * 128 : (c + 1) * 128] = x_f32[c, 0 : depth * lanes, :].astype(bf16)
    zero = jnp.zeros((gw, gw), bf16)

    pltpu.make_async_copy(flat_a.at[0], flat.at[slot], sems.at[slot]).wait()
    total = jnp.zeros((m, LANES), f32)
    for j in range(tiles):
        cols = []
        for b in range(TUP):
            taps_of = [TUP * j + a - b - (TUP - 1) for a in range(TUP)]
            cols.append(
                jnp.concatenate(
                    [
                        flat[slot, k * gw : (k + 1) * gw, 0:gw] if 0 <= k < taps else zero
                        for k in taps_of
                    ],
                    0,
                )
            )
        cols.append(jnp.zeros((n, LANES - n), bf16))
        total = total + dot(x_b[lanes * j : lanes * j + m, 0:n], jnp.concatenate(cols, 1))
    for i in range(2, groups):

        @pl.when(g == i - 2)
        def _(i=i):
            fetch(i)

    own = x_b[lanes * centre : lanes * centre + m, :].astype(f32)
    rows = [bias[...].reshape(1, -1)[:, i * gw : (i + 1) * gw] for i in range(groups)]
    gap = jnp.zeros((1, LANES - n), f32)
    shift = jnp.zeros((1, LANES), f32)
    for i in range(groups):
        shift = jnp.where(g == i, jnp.concatenate([rows[i]] * TUP + [gap], 1), shift)
    put(s_f32.at[g], 0, own + gelu(total + shift))

    @pl.when(g == groups - 1)
    def _():
        share = TUP * step
        for r in range(n_rec):
            for p in range(phases):
                rows = [take(s_f32.at[i], r * phases + p, step, lanes) for i in range(groups)]
                for b in range(TUP):
                    count = -(-(min(share, frames - p * share) - b) // TUP)
                    line = jnp.concatenate([v[:, b * gw : (b + 1) * gw] for v in rows], 1)
                    gap = plain.shape[0] * 128 - groups * gw
                    line = jnp.concatenate([line, jnp.zeros((step, gap), f32)], 1)
                    put(plain, r * frames + p * share + b, line[0:count], TUP)
        for r in range(n_rec):
            first = jnp.zeros((1, frames), f32)
            second = jnp.zeros((1, frames), f32)
            for c in range(plain.shape[0]):
                end = min(groups * gw, (c + 1) * 128)
                turned = plain[c, r * frames : (r + 1) * frames, :].T[0 : end - c * 128]
                summed[r, c * 128 : end, :] = turned
                first = first + jnp.sum(turned, 0, keepdims=True)
                second = second + jnp.sum(turned * turned, 0, keepdims=True)
            sums[r : r + 1, :] = first
            sums[n_rec + r : n_rec + r + 1, :] = second


def pos_conv(parts, flat_a, flat_b, bias, n_rec, frames, tiles, gw, centre):
    early = flat_a.shape[0]
    groups = early + flat_b.shape[0]
    phases = 16 // n_rec
    step = -(-(frames // phases) // TUP)
    depth = step + tiles
    tuples = parts[0].shape[1]
    lanes = 16
    width = groups * gw
    return pl.pallas_call(
        functools.partial(pos_conv_kernel, n_rec, early, phases, step, tiles, gw, frames, centre),
        grid=(groups,),
        in_specs=[
            *[pl.BlockSpec((1, tuples, LANES), lambda g: (g, 0, 0))] * n_rec,
            *[pl.BlockSpec(memory_space=pltpu.MemorySpace.HBM)] * 2,
            pl.BlockSpec(bias.shape, lambda g: (0,)),
        ],
        out_specs=[
            pl.BlockSpec((n_rec, width, frames), lambda g: (0, 0, 0)),
            pl.BlockSpec((2 * n_rec, frames), lambda g: (0, 0)),
        ],
        scratch_shapes=[
            pltpu.VMEM((2, *flat_a.shape[1:]), bf16),
            pltpu.VMEM((tuples + 16, LANES), f32),
            pltpu.VMEM((LANES // 128, (depth + 9) * lanes, 128), f32),
            pltpu.VMEM((depth * lanes, LANES), bf16),
            pltpu.VMEM((groups, LANES // 128, (step + 9) * lanes, 128), f32),
            pltpu.VMEM((-(-width // 128), n_rec * frames + 64, 128), f32),
            pltpu.SemaphoreType.DMA((2,)),
        ],
        out_shape=[
            jax.ShapeDtypeStruct((n_rec, width, frames), f32),
            jax.ShapeDtypeStruct((2 * n_rec, frames), f32),
        ],
        compiler_params=pltpu.CompilerParams(vmem_limit_bytes=48 * MIB),
        name="pos_conv",
    )(*parts, flat_a, flat_b, bias)


def on_device(
    features,
    conv5_weight,
    conv6_weight,
    conv7_weight,
    conv5_gain,
    conv6_gain,
    conv7_gain,
    proj_gain,
    proj_weight,
    proj_bias,
    pos_weight,
    pos_bias,
    out_gain,
    out_bias,
    lengths,
    crops,
):
    tm, grp = lax.axis_size("tm"), lax.axis_size("grp")
    groups, taps, gw, _ = pos_weight.shape
    half_kernel = taps // 2
    frames = features.shape[1] // 8
    crop = crops[0]

    back = [(i + 1, i) for i in range(tm - 1)]
    edge = lax.ppermute(features[:, :1, :], "tm", back)
    weights = (conv5_weight, conv6_weight, conv7_weight)
    gains = (conv5_gain, conv6_gain, conv7_gain, proj_gain)
    by_channel = pos_weight.transpose(0, 2, 3, 1)
    early = groups // 2
    normed, low, high = front(features, edge, weights, gains)

    start = crop - half_kernel
    piece = frames // 2
    pieces = jnp.floor_divide(start, piece)

    def from_block(distance):
        distance %= tm
        if distance == 0:
            return lambda v: v
        route = [((i + distance) % tm, i) for i in range(tm)]
        return lambda v: lax.ppermute(v, "tm", route)

    def branch(first):
        block, odd = first // 2, first % 2

        def run(v, low, high, w):
            pair = [from_block(block + odd + i)(v) for i in range(2)]
            extra = from_block(block)(high) if odd else from_block(block + 2)(low)
            return *pair, extra, by_tap(w, 0, early)

        return run

    tiles = -(-(taps + 2 * (TUP - 1)) // TUP)
    lowest = -(-half_kernel // piece)
    most = (frames * tm // 2 - 1 - half_kernel) // piece + 1
    *blocks, flat_a = lax.switch(
        pieces + lowest,
        [branch(b) for b in range(-lowest, most)],
        normed,
        low,
        high,
        by_channel,
    )

    n_rec = grp
    phases = 16 // n_rec
    step = -(-(frames // phases) // TUP)
    tuples = -(-(step * phases + tiles) // 8) * 8
    parts = project(
        blocks, proj_weight, proj_bias, crops, lengths, n_rec, groups, tuples, half_kernel
    )
    parts = [
        p if d == 0 else lax.ppermute(p, "grp", [(i ^ d, i) for i in range(grp)])
        for d, p in enumerate(parts)
    ]
    flat_b = by_tap(by_channel, early, groups - early)
    centre = (half_kernel + TUP - 1) // TUP
    summed, own = pos_conv(parts, flat_a, flat_b, pos_bias, n_rec, frames, tiles, gw, centre)
    totals = own
    for d in range(1, grp):
        totals = totals + lax.ppermute(own, "grp", [(i ^ d, i) for i in range(grp)])
    channels = proj_weight.shape[1]
    mean = totals[:n_rec] / channels
    spread = totals[n_rec:] / channels - mean * mean
    scaled = (summed - mean[:, None]) * lax.rsqrt(spread + epsilon)[:, None]
    scaled = scaled * out_gain[:, None] + out_bias[:, None]
    return scaled.astype(bf16).transpose(0, 2, 1)


def solution(mesh):
    return jax.shard_map(
        on_device,
        mesh=mesh,
        in_specs=(
            P("grp", "tm", None),
            P(),
            P(),
            P(),
            P(),
            P(),
            P(),
            P(),
            P(),
            P(),
            P("grp", None, None, None),
            P("grp"),
            P("grp"),
            P("grp"),
            P("grp"),
            P("grp"),
        ),
        out_specs=P(None, "tm", "grp"),
        check_vma=False,
    )
```

```python
import functools

import jax
import jax.numpy as jnp
from jax import lax
from jax.experimental import pallas as pl
from jax.experimental.pallas import tpu as pltpu
from jax.sharding import PartitionSpec as P

epsilon = 1e-05
f32 = jnp.float32
bf16 = jnp.bfloat16
TUP = 3
LANES = 256
MIB = 1 << 20


def gelu(x):
    return 0.5 * x * (1.0 + lax.erf(x * 0.7071067811865476))


def layer_norm(values, gain):
    centre = jnp.mean(values, -1, keepdims=True)
    centred = values - centre
    spread = jnp.mean(centred * centred, -1, keepdims=True)
    return centred * lax.rsqrt(spread + epsilon) * gain


def dot(a, b):
    return jnp.dot(a, b, preferred_element_type=f32)


def put(columns, first, value, stride=None):
    for c in range(columns.shape[0]):
        at = pl.ds(first, value.shape[0], stride=stride)
        columns[c, at, :] = value[:, c * 128 : (c + 1) * 128]


def take(columns, first, count, stride):
    return jnp.concatenate(
        [columns[c, pl.ds(first, count, stride=stride), :] for c in range(columns.shape[0])], 1
    )


def front_kernel(feat, nxt, w5, w6, w7, *refs):
    *gains, out, low, high, rows, block, v5, v6, v7, sems = refs
    gains = [g[...].reshape(1, -1) for g in gains]
    n = block.shape[0]
    f = n // 8
    sources = (feat.at[0], w5, w6, w7)
    copies = [
        pltpu.make_async_copy(source, target, sems.at[i])
        for i, (source, target) in enumerate(zip(sources, (block, v5, v6, v7)))
    ]
    for copy in copies:
        copy.start()
    copies[0].wait()
    put(rows, 0, block[...].astype(f32))
    put(rows, n, nxt[0].astype(f32))
    x = [take(rows, k, f, 8).astype(bf16) for k in range(9)]
    joined = jnp.concatenate(
        [jnp.concatenate(x[k : k + 7 : 2], 0) for k in range(3)], 1
    )
    copies[1].wait()
    h = gelu(layer_norm(dot(joined, v5[...]), gains[0])).astype(bf16)
    for layer, weight in ((1, v6), (2, v7)):
        count = h.shape[0] // f
        joined = jnp.concatenate(
            [
                jnp.concatenate([h[i * f : (i + 1) * f] for i in range(k, count, 2)], 0)
                for k in range(2)
            ],
            1,
        )
        copies[1 + layer].wait()
        h = gelu(layer_norm(dot(joined, weight[...]), gains[layer])).astype(bf16)
    normed = layer_norm(h.astype(f32), gains[3]).astype(bf16)
    out[...] = normed
    low[...] = normed[: f // 2]
    high[...] = normed[f // 2 :]


def front(features, nxt, weights, gains):
    rows, width = features.shape[1:]
    frames = rows // 8
    sizes = (frames, frames // 2, frames // 2)
    far = pl.BlockSpec(memory_space=pltpu.MemorySpace.HBM)
    flops = sum(2 * w.shape[0] * w.shape[1] * frames * m for w, m in zip(weights, (4, 2, 1)))
    return pl.pallas_call(
        front_kernel,
        grid=(1,),
        in_specs=[
            far,
            pl.BlockSpec(nxt.shape, lambda i: (0, 0, 0)),
            *[far] * 3,
            *[pl.BlockSpec(g.shape, lambda i: (0,)) for g in gains],
        ],
        out_specs=[pl.BlockSpec((n, width), lambda i: (0, 0)) for n in sizes],
        out_shape=[jax.ShapeDtypeStruct((n, width), bf16) for n in sizes],
        scratch_shapes=[
            pltpu.VMEM((width // 128, rows + 8, 128), f32),
            pltpu.VMEM((rows, width), bf16),
            *[pltpu.VMEM(w.shape, bf16) for w in weights],
            pltpu.SemaphoreType.DMA((4,)),
        ],
        cost_estimate=pl.CostEstimate(
            flops=4 * flops, transcendentals=0, bytes_accessed=8 * MIB
        ),
        name="front",
    )(features, nxt, *weights, *gains)


def project_kernel(n_dest, groups, tuples, half_kernel, crops, lengths, b0, b1, b2, w, bias, *rest):
    outs, rows = rest[:n_dest], rest[n_dest]
    frames = b0.shape[0]
    crop, length = crops[0], lengths[0]
    piece = b2.shape[0]
    rem = lax.rem(crop - half_kernel + 2 * half_kernel * frames, frames)
    odd = rem >= piece
    rem = jnp.where(odd, rem - piece, rem)
    first, total = lax.axis_index("tm") * frames, lax.axis_size("tm") * frames
    me = lax.axis_index("grp")
    rows[:, 0:8, :] = jnp.zeros((rows.shape[0], 8, 128), f32)
    at = pl.multiple_of(jnp.where(odd, 8 + piece, 8), 8)
    put(rows, at, b0[...].astype(f32))
    put(rows, pl.multiple_of(at + frames, 8), b1[...].astype(f32))
    put(rows, pl.multiple_of(jnp.where(odd, 8, 8 + 2 * frames), 8), b2[...].astype(f32))
    rows[:, 8 + 2 * frames + piece :, :] = jnp.zeros((rows.shape[0], 16, 128), f32)
    lead = TUP - 1
    parts = []
    for a in range(TUP):
        picked = take(rows, 8 - lead + a + rem, tuples, TUP).astype(bf16)
        value = dot(picked, w[...]) + bias[...].reshape(1, -1)
        x = TUP * lax.broadcasted_iota(jnp.int32, (tuples, 1), 0) + a
        j = first - half_kernel - lead + x
        s = j + crop
        s = jnp.where(s >= total, s - total, s)
        good = (x >= lead) & (x < lead + frames + 2 * half_kernel) & (j >= 0) & (j < total)
        good = good & (s < length)
        parts.append(jnp.where(good, value, 0.0).astype(bf16))
    width = w.shape[1] // n_dest
    gw = width // groups
    pad = jnp.zeros((tuples, LANES - TUP * gw), bf16)
    for dest in range(n_dest):
        pieces = []
        for g in range(groups):
            at = dest * width + g * gw
            pieces.append(
                jnp.concatenate([p[:, at : at + gw] for p in parts] + [pad], 1)
            )
        for d in range(n_dest):

            @pl.when(me == dest ^ d)
            def _(d=d, pieces=pieces):
                for g in range(groups):
                    outs[d][g] = pieces[g]


def project(blocks, w, bias, crops, lengths, n_dest, groups, tuples, half_kernel):
    frames, width = blocks[0].shape
    whole = lambda a: pl.BlockSpec(a.shape, lambda i, *s: (0,) * a.ndim)
    shape = (groups, tuples, LANES)
    return pl.pallas_call(
        functools.partial(project_kernel, n_dest, groups, tuples, half_kernel),
        grid_spec=pltpu.PrefetchScalarGridSpec(
            num_scalar_prefetch=2,
            grid=(1,),
            in_specs=[*[whole(b) for b in blocks], whole(w), whole(bias)],
            out_specs=[pl.BlockSpec(shape, lambda i, *s: (0, 0, 0))] * n_dest,
            scratch_shapes=[pltpu.VMEM((width // 128, 2 * frames + blocks[2].shape[0] + 24, 128), f32)],
        ),
        out_shape=[jax.ShapeDtypeStruct(shape, bf16)] * n_dest,
        compiler_params=pltpu.CompilerParams(vmem_limit_bytes=40 * MIB),
        name="project_window",
    )(crops, lengths, *blocks, w, bias)


def by_tap_kernel(w, out, wide):
    gw, taps = w.shape[1], w.shape[3]
    none = jnp.zeros((128 - gw, taps), f32)

    def one(i, carry):
        put(wide, i, jnp.concatenate([w[0, i].astype(f32), none], 0).T, gw)
        return carry

    lax.fori_loop(0, gw, one, 0, unroll=20)
    step = 4 * gw
    for first in range(0, taps * gw, step):
        out[0, first : first + step, :] = wide[0, first : first + step, :].astype(bf16)


def by_tap(by_channel, first, count):
    _, gw, _, taps = by_channel.shape
    return pl.pallas_call(
        by_tap_kernel,
        grid=(count,),
        in_specs=[pl.BlockSpec((1, gw, gw, taps), lambda g: (g + first, 0, 0, 0))],
        out_specs=pl.BlockSpec((1, taps * gw, 128), lambda g: (g, 0, 0)),
        out_shape=jax.ShapeDtypeStruct((count, taps * gw, 128), bf16),
        scratch_shapes=[pltpu.VMEM((1, taps * gw, 128), f32)],
        cost_estimate=pl.CostEstimate(
            flops=0, transcendentals=0, bytes_accessed=count * taps * gw * 128 * 8
        ),
        name="by_tap_%d" % first,
    )(by_channel)


def pos_conv_kernel(n_rec, early, phases, step, tiles, gw, frames, centre, *refs):
    parts, refs = refs[:n_rec], refs[n_rec:]
    flat_a, flat_b, bias, summed, sums, flat, wide, x_f32, x_b, s_f32, plain, sems = refs
    me = lax.axis_index("grp")
    taps = flat_a.shape[1] // gw
    groups = s_f32.shape[0]
    lanes = n_rec * phases
    depth = step + tiles
    m = step * lanes
    n = TUP * gw
    g = pl.program_id(0)
    slot = lax.rem(g, 2)

    def fetch(i):
        source = flat_a.at[i] if i < early else flat_b.at[i - early]
        pltpu.make_async_copy(source, flat.at[i % 2], sems.at[i % 2]).start()

    @pl.when(g == 0)
    def _():
        for i in range(min(2, groups)):
            fetch(i)

    for d in range(n_rec):
        wide[0 : parts[d].shape[1], :] = parts[d][0].astype(f32)
        rec = me ^ d
        for p in range(phases):
            put(x_f32, rec * phases + p, wide[p * step : p * step + depth, :], lanes)
    for c in range(LANES // 128):
        x_b[:, c * 128 : (c + 1) * 128] = x_f32[c, 0 : depth * lanes, :].astype(bf16)
    zero = jnp.zeros((gw, gw), bf16)

    pltpu.make_async_copy(flat_a.at[0], flat.at[slot], sems.at[slot]).wait()
    total = jnp.zeros((m, LANES), f32)
    for j in range(tiles):
        cols = []
        for b in range(TUP):
            taps_of = [TUP * j + a - b - (TUP - 1) for a in range(TUP)]
            cols.append(
                jnp.concatenate(
                    [
                        flat[slot, k * gw : (k + 1) * gw, 0:gw] if 0 <= k < taps else zero
                        for k in taps_of
                    ],
                    0,
                )
            )
        cols.append(jnp.zeros((n, LANES - n), bf16))
        total = total + dot(x_b[lanes * j : lanes * j + m, 0:n], jnp.concatenate(cols, 1))
    for i in range(2, groups):

        @pl.when(g == i - 2)
        def _(i=i):
            fetch(i)

    own = x_b[lanes * centre : lanes * centre + m, :].astype(f32)
    rows = [bias[...].reshape(1, -1)[:, i * gw : (i + 1) * gw] for i in range(groups)]
    gap = jnp.zeros((1, LANES - n), f32)
    shift = jnp.zeros((1, LANES), f32)
    for i in range(groups):
        shift = jnp.where(g == i, jnp.concatenate([rows[i]] * TUP + [gap], 1), shift)
    put(s_f32.at[g], 0, own + gelu(total + shift))

    @pl.when(g == groups - 1)
    def _():
        share = TUP * step
        for r in range(n_rec):
            for p in range(phases):
                rows = [take(s_f32.at[i], r * phases + p, step, lanes) for i in range(groups)]
                for b in range(TUP):
                    count = -(-(min(share, frames - p * share) - b) // TUP)
                    line = jnp.concatenate([v[:, b * gw : (b + 1) * gw] for v in rows], 1)
                    gap = plain.shape[0] * 128 - groups * gw
                    line = jnp.concatenate([line, jnp.zeros((step, gap), f32)], 1)
                    put(plain, r * frames + p * share + b, line[0:count], TUP)
        for r in range(n_rec):
            first = jnp.zeros((1, frames), f32)
            second = jnp.zeros((1, frames), f32)
            for c in range(plain.shape[0]):
                end = min(groups * gw, (c + 1) * 128)
                turned = plain[c, r * frames : (r + 1) * frames, :].T[0 : end - c * 128]
                summed[r, c * 128 : end, :] = turned
                first = first + jnp.sum(turned, 0, keepdims=True)
                second = second + jnp.sum(turned * turned, 0, keepdims=True)
            sums[r : r + 1, :] = first
            sums[n_rec + r : n_rec + r + 1, :] = second


def pos_conv(parts, flat_a, flat_b, bias, n_rec, frames, tiles, gw, centre):
    early = flat_a.shape[0]
    groups = early + flat_b.shape[0]
    phases = 16 // n_rec
    step = -(-(frames // phases) // TUP)
    depth = step + tiles
    tuples = parts[0].shape[1]
    lanes = 16
    width = groups * gw
    return pl.pallas_call(
        functools.partial(pos_conv_kernel, n_rec, early, phases, step, tiles, gw, frames, centre),
        grid=(groups,),
        in_specs=[
            *[pl.BlockSpec((1, tuples, LANES), lambda g: (g, 0, 0))] * n_rec,
            *[pl.BlockSpec(memory_space=pltpu.MemorySpace.HBM)] * 2,
            pl.BlockSpec(bias.shape, lambda g: (0,)),
        ],
        out_specs=[
            pl.BlockSpec((n_rec, width, frames), lambda g: (0, 0, 0)),
            pl.BlockSpec((2 * n_rec, frames), lambda g: (0, 0)),
        ],
        scratch_shapes=[
            pltpu.VMEM((2, *flat_a.shape[1:]), bf16),
            pltpu.VMEM((tuples + 16, LANES), f32),
            pltpu.VMEM((LANES // 128, (depth + 9) * lanes, 128), f32),
            pltpu.VMEM((depth * lanes, LANES), bf16),
            pltpu.VMEM((groups, LANES // 128, (step + 9) * lanes, 128), f32),
            pltpu.VMEM((-(-width // 128), n_rec * frames + 64, 128), f32),
            pltpu.SemaphoreType.DMA((2,)),
        ],
        out_shape=[
            jax.ShapeDtypeStruct((n_rec, width, frames), f32),
            jax.ShapeDtypeStruct((2 * n_rec, frames), f32),
        ],
        compiler_params=pltpu.CompilerParams(vmem_limit_bytes=48 * MIB),
        name="pos_conv",
    )(*parts, flat_a, flat_b, bias)


def on_device(
    features,
    conv5_weight,
    conv6_weight,
    conv7_weight,
    conv5_gain,
    conv6_gain,
    conv7_gain,
    proj_gain,
    proj_weight,
    proj_bias,
    pos_weight,
    pos_bias,
    out_gain,
    out_bias,
    lengths,
    crops,
):
    tm, grp = lax.axis_size("tm"), lax.axis_size("grp")
    groups, taps, gw, _ = pos_weight.shape
    half_kernel = taps // 2
    frames = features.shape[1] // 8
    crop = crops[0]

    back = [(i + 1, i) for i in range(tm - 1)]
    edge = lax.ppermute(features[:, :1, :], "tm", back)
    weights = (conv5_weight, conv6_weight, conv7_weight)
    gains = (conv5_gain, conv6_gain, conv7_gain, proj_gain)
    by_channel = pos_weight.transpose(0, 2, 3, 1)
    early = groups // 2
    normed, low, high = front(features, edge, weights, gains)

    start = crop - half_kernel
    piece = frames // 2
    pieces = jnp.floor_divide(start, piece)

    def from_block(distance):
        distance %= tm
        if distance == 0:
            return lambda v: v
        route = [((i + distance) % tm, i) for i in range(tm)]
        return lambda v: lax.ppermute(v, "tm", route)

    def branch(first):
        block, odd = first // 2, first % 2

        def run(v, low, high, w):
            pair = [from_block(block + odd + i)(v) for i in (1, 0)]
            extra = from_block(block)(high) if odd else from_block(block + 2)(low)
            return *pair, extra, by_tap(w, 0, early)

        return run

    tiles = -(-(taps + 2 * (TUP - 1)) // TUP)
    lowest = -(-half_kernel // piece)
    most = (frames * tm // 2 - 1 - half_kernel) // piece + 1
    *blocks, flat_a = lax.switch(
        pieces + lowest,
        [branch(b) for b in range(-lowest, most)],
        normed,
        low,
        high,
        by_channel,
    )
    blocks = (blocks[1], blocks[0], blocks[2])

    n_rec = grp
    phases = 16 // n_rec
    step = -(-(frames // phases) // TUP)
    tuples = -(-(step * phases + tiles) // 8) * 8
    parts = project(
        blocks, proj_weight, proj_bias, crops, lengths, n_rec, groups, tuples, half_kernel
    )
    parts = [
        p if d == 0 else lax.ppermute(p, "grp", [(i ^ d, i) for i in range(grp)])
        for d, p in enumerate(parts)
    ]
    flat_b = by_tap(by_channel, early, groups - early)
    centre = (half_kernel + TUP - 1) // TUP
    summed, own = pos_conv(parts, flat_a, flat_b, pos_bias, n_rec, frames, tiles, gw, centre)
    totals = own
    for d in range(1, grp):
        totals = totals + lax.ppermute(own, "grp", [(i ^ d, i) for i in range(grp)])
    channels = proj_weight.shape[1]
    mean = totals[:n_rec] / channels
    spread = totals[n_rec:] / channels - mean * mean
    scaled = (summed - mean[:, None]) * lax.rsqrt(spread + epsilon)[:, None]
    scaled = scaled * out_gain[:, None] + out_bias[:, None]
    return scaled.astype(bf16).transpose(0, 2, 1)


def solution(mesh):
    return jax.shard_map(
        on_device,
        mesh=mesh,
        in_specs=(
            P("grp", "tm", None),
            P(),
            P(),
            P(),
            P(),
            P(),
            P(),
            P(),
            P(),
            P(),
            P("grp", None, None, None),
            P("grp"),
            P("grp"),
            P("grp"),
            P("grp"),
            P("grp"),
        ),
        out_specs=P(None, "tm", "grp"),
        check_vma=False,
    )
```
